32 devices in a mesh: groups: 2 (over x), ind: 16 (over z, y, core).
Axes of the slice: x: 2, y: 2, z: 4, core: 2. Of those that a mesh axis runs over, the one named last changes fastest.
Arguments:
- genotype: bfloat16 [12288, 16384], P(('groups', 'ind')), parts along dimension 0, may hold values from -4 to 4
- residual: bfloat16 [12288, 256], P(('groups', 'ind')), parts along dimension 0, may hold values from -4 to 4
- labels: int32 [12288, 256], P(('groups', 'ind')), parts along dimension 0, may hold values 0 or 1
- incl_old: float32 [32768, 256], P(('groups', 'ind')), parts along dimension 0, may hold values from 0.02 to 0.98
- mean_old: float32 [32768, 256], P(('groups', 'ind')), parts along dimension 0, may hold values from -0.078125 to 0.078125
- prior_logit: float32 [256], replicated, may hold values from -4 to 0
- slab_scale: float32 [256], replicated, may hold values from 0.25 to 8
- offset: float32 [256], replicated, may hold values from -2 to 1
Outputs:
- incl_new: float32 [32768, 256], P(('groups', 'ind')), parts along dimension 0
- mean_new: float32 [32768, 256], P(('groups', 'ind')), parts along dimension 0
- resid_new: float32 [12288, 256], P(('groups', 'ind')), parts along dimension 0
The draws below stay inside these ranges and needn't reach their ends.
There are 2 independent parts, one for each index of `groups`. The reference program is written for one: setup_inputs(seed, part) draws one part's arguments, and reference() takes and returns one part's arrays. A program takes and returns all parts, laid end to end along the dimension named above; an argument that names none is the same for every part. Nothing has to cross between parts.
All inputs are finite; a program needn't handle non-finite values. No bound on the sum of `labels` on one device may be relied on, other than what follows from the above.
Results may differ from the reference program's by a relative error of at most 0.00062.
Values may be sent and summed in bfloat16 or wider, within the bound.
A program may use at most 128 MiB of HBM per device.

```python
import math
import jax
import jax.numpy as jnp

NVAR = 16384
COLS = 256
NIND = 6144


def with_ends(entries, own_key, least, top_value):
    shape = entries.shape
    index_at = [jax.random.randint(jax.random.fold_in(own_key, axis), (), 0, shape[axis]) for axis in range(len(shape))]
    entries = entries.at[tuple(index_at)].set(least)
    longest = shape.index(max(shape))
    index_at[longest] = (index_at[longest] + 1) % shape[longest]
    return entries.at[tuple(index_at)].set(top_value)


def spiked(result, own_key, source, target, blocks, factor):
    def block_of(axis_at):
        return (jnp.arange(result.shape[axis_at]) // (result.shape[axis_at] // blocks)).reshape((-1,) + (1,) * (result.ndim - 1 - axis_at))

    one_side = jax.random.permutation(own_key, blocks)[block_of(target)]
    other_side = (block_of(target) + blocks // 2) % blocks
    return jnp.where((block_of(source) == one_side) | (block_of(source) == other_side), factor * result, result)


def shard_levels(key, dims, cuts, low, largest):
    level, own = 1.0, jax.random.fold_in(key, 6)
    for axis_at, shards_of in cuts:
        draws = jnp.exp(jax.random.uniform(jax.random.fold_in(own, axis_at), (shards_of,), jnp.float32, low / len(cuts), largest / len(cuts)))
        level = level * jnp.repeat(draws, dims[axis_at] // shards_of).reshape([-1 if axis == axis_at else 1 for axis in range(len(dims))])
    return level


def centred(own_key, shape, spread, bound, split=(), held_as=jnp.bfloat16):
    values = spread * jax.random.normal(own_key, shape, jnp.float32)
    if split:
        values = values * shard_levels(own_key, shape, split, -0.22, 0.18)
    return jnp.clip(values, -bound, bound).astype(held_as)


def heavy_noise(key, shape, scale, reach, cuts, heavy, dtype=jnp.bfloat16):
    drawn = scale * jax.random.normal(key, shape, jnp.float32)
    if cuts:
        drawn = drawn * shard_levels(key, shape, cuts, -0.22, 0.18)
    return jnp.clip(spiked(drawn, jax.random.fold_in(key, 3), *heavy), -reach, reach).astype(dtype)


def setup_inputs(seed: int = 0, part: int = 0) -> dict:
    arg_keys = jax.random.split(jax.random.key(seed), 9)
    part_splits = jax.random.split(jax.random.fold_in(arg_keys[8], part), 9)
    genotype = heavy_noise(part_splits[0], (NIND, NVAR), 1.0, 4.0, ((0, 16),), (0, 1, 16, 2.0))
    residual = centred(part_splits[1], (NIND, COLS), 1.5, 4.0, ((0, 16),))
    labels = with_ends((jax.random.randint(part_splits[2], (NIND, COLS), 0, 2) < 1).astype(jnp.int32), jax.random.fold_in(part_splits[2], 1), 0, 1)
    incl_old = jnp.clip(0.02 + 0.96000002 * jax.random.uniform(part_splits[3], (NVAR, COLS), jnp.float32) ** shard_levels(part_splits[3], (NVAR, COLS), ((0, 16),), -0.2, 0.2), 0.02, 0.98)
    mean_old = centred(part_splits[4], (NVAR, COLS), NIND ** -0.5, 0.078125, ((0, 16),), jnp.float32)
    prior_logit = jnp.clip(jax.random.uniform(arg_keys[5], (COLS,), jnp.float32, -4.0, 0.0), -4.0, 0.0)
    slab_scale = jnp.clip(jnp.exp(jax.random.uniform(arg_keys[6], (COLS,), jnp.float32, math.log(0.25), math.log(8.0))), 0.25, 8.0)
    offset = jnp.clip(jax.random.uniform(arg_keys[7], (COLS,), jnp.float32, -2.0, 1.0), -2.0, 1.0)
    return dict(genotype=genotype, residual=residual, labels=labels, incl_old=incl_old, mean_old=mean_old, prior_logit=prior_logit, slab_scale=slab_scale, offset=offset)


def reference(genotype, residual, labels, incl_old, mean_old, prior_logit, slab_scale, offset):
    corr = jnp.dot(genotype.T, residual, preferred_element_type=jnp.float32)
    stat = corr / NIND + incl_old * mean_old
    shrink = slab_scale / (1.0 + slab_scale)
    mean_new = stat * shrink
    logit = prior_logit - 0.5 * jnp.log1p(slab_scale) + 0.5 * NIND * shrink * stat * stat
    incl_new = 0.5 * incl_old + 0.5 * jax.nn.sigmoid(logit)
    effect = (incl_new * mean_new).astype(jnp.bfloat16)
    eta = jnp.dot(genotype, effect, preferred_element_type=jnp.float32) + offset
    resid_new = 4.0 * (labels.astype(jnp.float32) - jax.nn.sigmoid(eta))
    return incl_new, mean_new, resid_new
```

```python
import functools
import math

import jax
import jax.numpy as jnp
from jax import lax
from jax.experimental import pallas as pl
from jax.experimental.pallas import tpu as pltpu
from jax.sharding import PartitionSpec as P

LARGEST_TERM = 64.0


def sweep_kernel(
    n, chunks,
    geno_hbm, resid_ref, labels_hbm, incl_hbm, mean_hbm, prior_ref, scale_ref, offset_ref,
    incl_out, mean_out, resid_out,
    geno, labels, incl, mean, core_out, core_in, pair_out, pair_in, own, line_out, line_in, eff, eta,
    geno_sem, in_sem, core_ss, core_rs, pair_ss, pair_rs, line_ss, line_rs,
    gz_ss, gz_rs, gy_ss, gy_rs, gc_ss, gc_rs,
):
    length = n // 4
    owned = incl.shape[0]
    rows = owned // chunks
    people = geno.shape[0]
    total = float(people * n)
    coding = 32760.0 / math.log(1.0 + LARGEST_TERM * total)
    me = lax.axis_index("ind")
    z = me // 4
    y = (me // 2) % 2
    c = me % 2

    def at(zz, yy, cc):
        return zz * 4 + yy * 2 + cc

    core_dev = {"ind": at(z, y, 1 - c)}
    pair_dev = {"ind": at(z, 1 - y, c)}
    up_dev = {"ind": at(lax.rem(z + 1, length), y, c)}
    down_dev = {"ind": at(lax.rem(z + length - 1, length), y, c)}
    has_up = z < length - 1
    has_down = z > 0

    def remote(src, dst, ss, rs, dev):
        return pltpu.make_async_remote_copy(
            src_ref=src, dst_ref=dst, send_sem=ss, recv_sem=rs,
            device_id=dev, device_id_type=pl.DeviceIdType.MESH,
        )

    def encode(x):
        code = (jnp.log(1.0 + jnp.abs(x)) * coding + 0.5).astype(jnp.int32)
        return jnp.where(x < 0.0, -code, code).astype(jnp.int16)

    def decode(code):
        level = code.astype(jnp.int32).astype(jnp.float32)
        size = jnp.exp(jnp.abs(level) * (1.0 / coding)) - 1.0
        return jnp.where(level < 0.0, -size, size)

    def cols(s, o):
        return pl.ds(pl.multiple_of(o * owned + s * rows, 128), rows)

    def load(s, o):
        return pltpu.make_async_copy(
            geno_hbm.at[:, cols(s, o)], geno.at[:, cols(s, o)], geno_sem.at[s, o]
        )

    def for_z(body):
        lax.fori_loop(0, length, lambda i, _: (body(i), 0)[1], 0)

    def loop(count, body):
        lax.fori_loop(0, count, lambda i, _: (body(i), 0)[1], 0)

    owners = ((1 - y, 1 - c), (y, 1 - c), (y, c), (1 - y, c))

    def load_chunk(s):
        for yy, cc in owners:
            for_z(lambda i: load(s, at(i, yy, cc)).start())

    loop(chunks, load_chunk)
    small = [
        pltpu.make_async_copy(labels_hbm, labels, in_sem.at[0]),
        pltpu.make_async_copy(incl_hbm, incl, in_sem.at[1]),
        pltpu.make_async_copy(mean_hbm, mean, in_sem.at[2]),
    ]
    for copy in small:
        copy.start()

    barrier = pltpu.get_barrier_semaphore()
    pl.semaphore_signal(barrier, inc=1, device_id=core_dev, device_id_type=pl.DeviceIdType.MESH)
    pl.semaphore_signal(barrier, inc=1, device_id=pair_dev, device_id_type=pl.DeviceIdType.MESH)

    @pl.when(has_up)
    def _():
        pl.semaphore_signal(barrier, inc=1, device_id=up_dev, device_id_type=pl.DeviceIdType.MESH)

    @pl.when(has_down)
    def _():
        pl.semaphore_signal(barrier, inc=1, device_id=down_dev, device_id_type=pl.DeviceIdType.MESH)

    pl.semaphore_wait(barrier, 2 + has_up.astype(jnp.int32) + has_down.astype(jnp.int32))

    def product(s, o):
        load(s, o).wait()
        return lax.dot_general(
            geno[:, cols(s, o)], resid_ref[...], (((0,), (0,)), ((), ())),
            preferred_element_type=jnp.float32,
        )

    def core_copy(s, h):
        return remote(core_out.at[s, h], core_in.at[s, h], core_ss.at[s, h], core_rs.at[s, h], core_dev)

    def pair_copy(s):
        return remote(pair_out.at[s], pair_in.at[s], pair_ss.at[s], pair_rs.at[s], pair_dev)

    def line_copy(s, t, d):
        return remote(
            line_out.at[s, t, d], line_in.at[s, t, d], line_ss.at[s, t, d], line_rs.at[s, t, d],
            up_dev if d == 0 else down_dev,
        )

    def first(s):
        for h in range(2):
            yy, cc = owners[h]

            def part(i):
                core_out[s, h, i] = product(s, at(i, yy, cc))

            for_z(part)
            core_copy(s, h).start()

        def keep(i):
            own[s, i] = product(s, at(i, y, c))

        for_z(keep)
        core_copy(s, 0).wait_recv()

        def pass_on(i):
            pair_out[s, i] = encode(product(s, at(i, 1 - y, c)) + core_in[s, 0, i])

        for_z(pass_on)
        pair_copy(s).start()

    loop(chunks, first)
    for copy in small:
        copy.wait()
    eta[...] = jnp.zeros_like(eta)

    scale = scale_ref[...]
    shrink = scale / (1.0 + scale)
    bias = prior_ref[...] - 0.5 * jnp.log1p(scale)
    curve = 0.5 * total * shrink

    def along(s, t):
        @pl.when(t == 0)
        def _():
            core_copy(s, 1).wait_recv()
            pair_copy(s).wait_recv()

            def add(i):
                own[s, i] = own[s, i] + core_in[s, 1, i] + decode(pair_in[s, i])

            for_z(add)

        for d in range(2):
            place = z if d == 0 else length - 1 - z
            block = length - 1 - t + z if d == 0 else t - (length - 1 - z)

            @pl.when((place <= t) & (place < length - 1))
            def _():
                @pl.when(place == 0)
                def _():
                    line_out[s, t, d] = encode(own[s, block])

                @pl.when(place > 0)
                def _():
                    line_copy(s, t - 1, d).wait_recv()
                    line_out[s, t, d] = encode(own[s, block] + decode(line_in[s, t - 1, d]))

                line_copy(s, t, d).start()

    def gz_copy(s, u, d):
        o = at(z - u if d == 0 else z + u, y, c)
        return remote(
            eff.at[s, o], eff.at[s, o], gz_ss.at[s, u, d], gz_rs.at[s, u, d], up_dev if d == 0 else down_dev
        )

    def gz_landed(s, u, d):
        o = at(z - 1 - u if d == 0 else z + 1 + u, y, c)
        return remote(
            eff.at[s, o], eff.at[s, o], gz_ss.at[s, u, d], gz_rs.at[s, u, d], up_dev if d == 0 else down_dev
        )

    def gy_copy(s, i, yy):
        o = at(i, yy, c)
        return remote(eff.at[s, o], eff.at[s, o], gy_ss.at[s, i], gy_rs.at[s, i], pair_dev)

    def gc_copy(s, i, yy, cc):
        o = at(i, yy, cc)
        return remote(eff.at[s, o], eff.at[s, o], gc_ss.at[s, yy, i], gc_rs.at[s, yy, i], core_dev)

    def use(s, o):
        eta[...] += jnp.dot(geno[:, cols(s, o)], eff[s, o], preferred_element_type=jnp.float32)

    def finish(s):
        for d in range(2):
            @pl.when(has_down if d == 0 else has_up)
            def _():
                line_copy(s, length - 2, d).wait_recv()
                own[s, z] = own[s, z] + decode(line_in[s, length - 2, d])

        here = pl.ds(pl.multiple_of(s * rows, 8), rows)
        before = incl[here, :]
        stat = own[s, z] / total + before * mean[here, :]
        mean_new = stat * shrink
        incl_new = 0.5 * before + 0.5 * jax.nn.sigmoid(bias + curve * stat * stat)
        mean_out[here, :] = mean_new
        incl_out[here, :] = incl_new
        eff[s, me] = (incl_new * mean_new).astype(jnp.bfloat16)

        @pl.when(has_up)
        def _():
            gz_copy(s, 0, 0).start()

        @pl.when(has_down)
        def _():
            gz_copy(s, 0, 1).start()

        gy_copy(s, z, y).start()
        gc_copy(s, z, y, c).start()
        use(s, me)

    def spread(s, u):
        for d in range(2):
            source = z - u if d == 0 else z + u

            @pl.when((source >= 0) & (source < length))
            def _():
                gz_landed(s, u - 1, d).wait_recv()

                @pl.when(has_up if d == 0 else has_down)
                def _():
                    gz_copy(s, u, d).start()

                gy_copy(s, source, y).start()
                gc_copy(s, source, y, c).start()
                use(s, at(source, y, c))

    def wave(w):
        def gather_step(k):
            u = length - 1 - k
            s = w - (length - 1) - u

            @pl.when((s >= 0) & (s < chunks))
            def _():
                spread(s, u)

        loop(length - 1, gather_step)
        s_now = w - (length - 1)

        @pl.when((s_now >= 0) & (s_now < chunks))
        def _():
            finish(s_now)

        def reduce_step(k):
            t = length - 2 - k
            s = w - t

            @pl.when((s >= 0) & (s < chunks))
            def _():
                along(s, t)

        loop(length - 1, reduce_step)

    loop(chunks + 2 * length - 2, wave)

    def from_core(s):
        def take(i):
            for yy in range(2):
                gc_copy(s, i, yy, 1 - c).wait_recv()
                use(s, at(i, yy, 1 - c))

        for_z(take)

    def last(s):
        def take(i):
            gy_copy(s, i, 1 - y).wait_recv()
            gc_copy(s, i, 1 - y, c).start()
            use(s, at(i, 1 - y, c))

        for_z(take)

        @pl.when(s > 0)
        def _():
            from_core(s - 1)

    loop(chunks, last)
    from_core(chunks - 1)

    resid_out[...] = 4.0 * (
        labels[...].astype(jnp.float32) - jax.nn.sigmoid(eta[...] + offset_ref[...])
    )

    def drain(s):
        for h in range(2):
            core_copy(s, h).wait_send()
        pair_copy(s).wait_send()

        def step(t):
            for d in range(2):
                place = z if d == 0 else length - 1 - z
                origin = z - t if d == 0 else z + t

                @pl.when((place <= t) & (place < length - 1))
                def _():
                    line_copy(s, t, d).wait_send()

                @pl.when((origin >= 0) & (origin < length) & (place < length - 1))
                def _():
                    gz_copy(s, t, d).wait_send()

        loop(length - 1, step)

        def blocks(i):
            gy_copy(s, i, y).wait_send()
            for yy in range(2):
                gc_copy(s, i, yy, c).wait_send()

        for_z(blocks)

    loop(chunks, drain)


def on_device(genotype, residual, labels, incl_old, mean_old, prior_logit, slab_scale, offset):
    n = lax.axis_size("ind")
    people, _ = genotype.shape
    owned, columns = incl_old.shape
    length = n // 4
    chunks = max(1, min(4, owned // 256))
    rows = owned // chunks
    f32, bf16, i16 = jnp.float32, jnp.bfloat16, jnp.int16
    anywhere = pl.BlockSpec(memory_space=pl.ANY)
    vmem = pl.BlockSpec(memory_space=pltpu.VMEM)
    dma = pltpu.SemaphoreType.DMA
    hops = length - 1
    return pl.pallas_call(
        functools.partial(sweep_kernel, n, chunks),
        out_shape=(
            jax.ShapeDtypeStruct((owned, columns), f32),
            jax.ShapeDtypeStruct((owned, columns), f32),
            jax.ShapeDtypeStruct((people, columns), f32),
        ),
        in_specs=[anywhere, vmem, anywhere, anywhere, anywhere, vmem, vmem, vmem],
        out_specs=(vmem, vmem, vmem),
        scratch_shapes=[
            pltpu.VMEM(genotype.shape, bf16),
            pltpu.VMEM(labels.shape, labels.dtype),
            pltpu.VMEM(incl_old.shape, f32),
            pltpu.VMEM(mean_old.shape, f32),
            pltpu.VMEM((chunks, 2, length, rows, columns), f32),
            pltpu.VMEM((chunks, 2, length, rows, columns), f32),
            pltpu.VMEM((chunks, length, rows, columns), i16),
            pltpu.VMEM((chunks, length, rows, columns), i16),
            pltpu.VMEM((chunks, length, rows, columns), f32),
            pltpu.VMEM((chunks, hops, 2, rows, columns), i16),
            pltpu.VMEM((chunks, hops, 2, rows, columns), i16),
            pltpu.VMEM((chunks, n, rows, columns), bf16),
            pltpu.VMEM((people, columns), f32),
            dma((chunks, n)),
            dma((3,)),
            dma((chunks, 2)),
            dma((chunks, 2)),
            dma((chunks,)),
            dma((chunks,)),
            dma((chunks, hops, 2)),
            dma((chunks, hops, 2)),
            dma((chunks, hops, 2)),
            dma((chunks, hops, 2)),
            dma((chunks, length)),
            dma((chunks, length)),
            dma((chunks, 2, length)),
            dma((chunks, 2, length)),
        ],
        compiler_params=pltpu.CompilerParams(
            collective_id=0, has_side_effects=True, vmem_limit_bytes=67043328
        ),
        name="sweep",
    )(
        genotype, residual, labels, incl_old, mean_old,
        prior_logit.reshape(1, -1), slab_scale.reshape(1, -1), offset.reshape(1, -1),
    )


def solution(mesh):
    placed = (
        P(("groups", "ind"), None),
        P(("groups", "ind"), None),
        P(("groups", "ind"), None),
        P(("groups", "ind"), None),
        P(("groups", "ind"), None),
        P(),
        P(),
        P(),
    )
    return jax.shard_map(
        on_device,
        mesh=mesh,
        in_specs=placed,
        out_specs=(
            P(("groups", "ind"), None),
            P(("groups", "ind"), None),
            P(("groups", "ind"), None),
        ),
        check_vma=False,
    )
```

```python
import functools
import math

import jax
import jax.numpy as jnp
from jax import lax
from jax.experimental import pallas as pl
from jax.experimental.pallas import tpu as pltpu
from jax.sharding import PartitionSpec as P

LARGEST_TERM = 64.0


def sweep_kernel(
    n, chunks, period,
    geno_hbm, resid_ref, incl_hbm, mean_hbm, prior_ref, scale_ref,
    stat_out, eta,
    geno, incl, mean, core_out, core_in, pair_out, pair_in, own, line_out, line_in, eff,
    geno_sem, in_sem, core_ss, core_rs, pair_ss, pair_rs, line_ss, line_rs,
    gz_ss, gz_rs, gy_ss, gy_rs, gc_ss, gc_rs,
):
    length = n // 4
    owned = incl.shape[0]
    rows = owned // chunks
    people = geno.shape[0]
    total = float(people * n)
    coding = 32760.0 / math.log(1.0 + LARGEST_TERM * total)
    me = lax.axis_index("ind")
    z = me // 4
    y = (me // 2) % 2
    c = me % 2

    def at(zz, yy, cc):
        return zz * 4 + yy * 2 + cc

    core_dev = {"ind": at(z, y, 1 - c)}
    pair_dev = {"ind": at(z, 1 - y, c)}
    up_dev = {"ind": at(lax.rem(z + 1, length), y, c)}
    down_dev = {"ind": at(lax.rem(z + length - 1, length), y, c)}
    has_up = z < length - 1
    has_down = z > 0

    def remote(src, dst, ss, rs, dev):
        return pltpu.make_async_remote_copy(
            src_ref=src, dst_ref=dst, send_sem=ss, recv_sem=rs,
            device_id=dev, device_id_type=pl.DeviceIdType.MESH,
        )

    def encode(x):
        code = (jnp.log(1.0 + jnp.abs(x)) * coding + 0.5).astype(jnp.int32)
        return jnp.where(x < 0.0, -code, code).astype(jnp.int16)

    def decode(code):
        level = code.astype(jnp.int32).astype(jnp.float32)
        size = jnp.exp(jnp.abs(level) * (1.0 / coding)) - 1.0
        return jnp.where(level < 0.0, -size, size)

    def cols(s, o):
        return pl.ds(pl.multiple_of(o * owned + s * rows, 128), rows)

    def load(s, o):
        return pltpu.make_async_copy(
            geno_hbm.at[:, cols(s, o)], geno.at[:, cols(s, o)], geno_sem.at[s, o]
        )

    def for_z(body):
        lax.fori_loop(0, length, lambda i, _: (body(i), 0)[1], 0)

    def loop(count, body):
        lax.fori_loop(0, count, lambda i, _: (body(i), 0)[1], 0)

    owners = ((1 - y, 1 - c), (y, 1 - c), (y, c), (1 - y, c))

    def load_chunk(s):
        for yy, cc in owners:
            for_z(lambda i: load(s, at(i, yy, cc)).start())

    loop(chunks, load_chunk)
    small = [
        pltpu.make_async_copy(incl_hbm, incl, in_sem.at[0]),
        pltpu.make_async_copy(mean_hbm, mean, in_sem.at[1]),
    ]
    for copy in small:
        copy.start()

    barrier = pltpu.get_barrier_semaphore()
    pl.semaphore_signal(barrier, inc=1, device_id=core_dev, device_id_type=pl.DeviceIdType.MESH)
    pl.semaphore_signal(barrier, inc=1, device_id=pair_dev, device_id_type=pl.DeviceIdType.MESH)

    @pl.when(has_up)
    def _():
        pl.semaphore_signal(barrier, inc=1, device_id=up_dev, device_id_type=pl.DeviceIdType.MESH)

    @pl.when(has_down)
    def _():
        pl.semaphore_signal(barrier, inc=1, device_id=down_dev, device_id_type=pl.DeviceIdType.MESH)

    pl.semaphore_wait(barrier, 2 + has_up.astype(jnp.int32) + has_down.astype(jnp.int32))

    def product(s, o):
        load(s, o).wait()
        return lax.dot_general(
            geno[:, cols(s, o)], resid_ref[...], (((0,), (0,)), ((), ())),
            preferred_element_type=jnp.float32,
        )

    def line_first(s):
        return lax.rem(s, period) == 0 if period else s < 0

    def flows(s):
        return 1 + line_first(s).astype(jnp.int32) if period else 1

    def slot(s, f):
        if not period:
            return s
        k = lax.rem(s, period)
        return (s // period) * (period + 1) + k + jnp.where(k == 0, f, 1)

    def side(f):
        return jnp.where(f == 0, y, 1 - y)

    def core_copy(s, h):
        return remote(
            core_out.at[s % 2, h], core_in.at[s, h], core_ss.at[s, h], core_rs.at[s, h], core_dev
        )

    def pair_copy(s):
        return remote(pair_out.at[s], pair_in.at[s], pair_ss.at[s], pair_rs.at[s], pair_dev)

    def pair_one(s):
        return remote(
            pair_out.at[s, 0], pair_in.at[s, 0], pair_ss.at[s], pair_rs.at[s], pair_dev
        )

    def line_copy(s, t, d, f):
        k = slot(s, f)
        return remote(
            line_out.at[k, t, d], line_in.at[k, t, d], line_ss.at[k, t, d], line_rs.at[k, t, d],
            up_dev if d == 0 else down_dev,
        )

    def first(s):
        for h in range(2):
            yy, cc = owners[h]

            @pl.when(s >= 2)
            def _():
                core_copy(s - 2, h).wait_send()

            def part(i):
                core_out[s % 2, h, i] = product(s, at(i, yy, cc))

            for_z(part)
            core_copy(s, h).start()

        def keep(i):
            own[slot(s, 0), i] = product(s, at(i, y, c))

        for_z(keep)

        @pl.when(line_first(s))
        def _():
            def keep_other(i):
                own[slot(s, 1), i] = product(s, at(i, 1 - y, c))

            for_z(keep_other)

        @pl.when(jnp.logical_not(line_first(s)))
        def _():
            core_copy(s, 0).wait_recv()

            def pass_on(i):
                pair_out[s, i] = encode(product(s, at(i, 1 - y, c)) + core_in[s, 0, i])

            for_z(pass_on)
            pair_copy(s).start()

    loop(chunks, first)
    for copy in small:
        copy.wait()
    eta[...] = jnp.zeros_like(eta)

    scale = scale_ref[...]
    shrink = scale / (1.0 + scale)
    bias = prior_ref[...] - 0.5 * jnp.log1p(scale)
    curve = 0.5 * total * shrink

    def settle(s):
        core_copy(s, 1).wait_recv()

        @pl.when(line_first(s))
        def _():
            core_copy(s, 0).wait_recv()

            def add(i):
                for f in range(2):
                    k = slot(s, f)
                    own[k, i] = own[k, i] + core_in[s, 1 - f, i]

            for_z(add)

        @pl.when(jnp.logical_not(line_first(s)))
        def _():
            pair_copy(s).wait_recv()

            def add(i):
                k = slot(s, 0)
                own[k, i] = own[k, i] + core_in[s, 1, i] + decode(pair_in[s, i])

            for_z(add)

    def along(s, t):
        @pl.when(t == 0)
        def _():
            settle(s)

        def flow(f):
            k = slot(s, f)
            for d in range(2):
                place = z if d == 0 else length - 1 - z
                block = length - 1 - t + z if d == 0 else t - (length - 1 - z)

                @pl.when((place <= t) & (place < length - 1))
                def _():
                    @pl.when(place == 0)
                    def _():
                        line_out[k, t, d] = encode(own[k, block])

                    @pl.when(place > 0)
                    def _():
                        line_copy(s, t - 1, d, f).wait_recv()
                        line_out[k, t, d] = encode(own[k, block] + decode(line_in[k, t - 1, d]))

                    line_copy(s, t, d, f).start()

        loop(flows(s), flow)

    def gz_copy(s, u, d, f):
        k, o = slot(s, f), at(z - u if d == 0 else z + u, side(f), c)
        return remote(
            eff.at[s, o], eff.at[s, o], gz_ss.at[k, u, d], gz_rs.at[k, u, d], up_dev if d == 0 else down_dev
        )

    def gz_landed(s, u, d, f):
        k, o = slot(s, f), at(z - 1 - u if d == 0 else z + 1 + u, side(f), c)
        return remote(
            eff.at[s, o], eff.at[s, o], gz_ss.at[k, u, d], gz_rs.at[k, u, d], up_dev if d == 0 else down_dev
        )

    def gy_copy(s, i, yy):
        o = at(i, yy, c)
        return remote(eff.at[s, o], eff.at[s, o], gy_ss.at[s, i], gy_rs.at[s, i], pair_dev)

    def gc_copy(s, i, yy, cc):
        o = at(i, yy, cc)
        return remote(eff.at[s, o], eff.at[s, o], gc_ss.at[s, yy, i], gc_rs.at[s, yy, i], core_dev)

    def use(s, o):
        eta[...] += jnp.dot(geno[:, cols(s, o)], eff[s, o], preferred_element_type=jnp.float32)

    def send_own(s, f):
        @pl.when(has_up)
        def _():
            gz_copy(s, 0, 0, f).start()

        @pl.when(has_down)
        def _():
            gz_copy(s, 0, 1, f).start()

        gc_copy(s, z, side(f), c).start()

    def total_of_line(s):
        def flow(f):
            k = slot(s, f)
            for d in range(2):
                @pl.when(has_down if d == 0 else has_up)
                def _():
                    line_copy(s, length - 2, d, f).wait_recv()
                    own[k, z] = own[k, z] + decode(line_in[k, length - 2, d])

        loop(flows(s), flow)

        @pl.when(line_first(s))
        def _():
            pair_out[s, 0] = encode(own[slot(s, 1), z])
            pair_one(s).start()

        @pl.when(jnp.logical_not(line_first(s)))
        def _():
            finish(s)

    def total_of_pair(s):
        pair_one(s).wait_recv()
        own[slot(s, 0), z] = own[slot(s, 0), z] + decode(pair_in[s, 0])
        finish(s)

    def finish(s):
        here = pl.ds(pl.multiple_of(s * rows, 8), rows)
        before = incl[here, :]
        stat = own[slot(s, 0), z] / total + before * mean[here, :]
        stat_out[here, :] = stat
        incl_new = 0.5 * before + 0.5 * jax.nn.sigmoid(bias + curve * stat * stat)
        eff[s, me] = (incl_new * (stat * shrink)).astype(jnp.bfloat16)
        gy_copy(s, z, y).start()
        send_own(s, 0)
        use(s, me)

    def send_other(s):
        gy_copy(s, z, 1 - y).wait_recv()
        send_own(s, 1)
        use(s, at(z, 1 - y, c))

    def spread(s, u, f):
        for d in range(2):
            source = z - u if d == 0 else z + u

            @pl.when((source >= 0) & (source < length))
            def _():
                gz_landed(s, u - 1, d, f).wait_recv()

                @pl.when(has_up if d == 0 else has_down)
                def _():
                    gz_copy(s, u, d, f).start()

                @pl.when(jnp.logical_not(line_first(s)))
                def _():
                    gy_copy(s, source, y).start()

                gc_copy(s, source, side(f), c).start()
                use(s, at(source, side(f), c))

    def within(s):
        return (s >= 0) & (s < chunks)

    def wave(w):
        def gather_step(k):
            u = length - 1 - k
            kinds = [(w - (length - 1) - u, 0, False)]
            if period:
                kinds = [(w - length - 1 - u, 1, True), (w - length - u, 0, True)] + kinds
            for s, f, kind in kinds:
                @pl.when(within(s) & (line_first(s) if kind else jnp.logical_not(line_first(s))))
                def _():
                    spread(s, u, f)

        loop(length - 1, gather_step)
        if period:
            @pl.when(within(w - length - 1) & line_first(w - length - 1))
            def _():
                send_other(w - length - 1)

            @pl.when(within(w - length) & line_first(w - length))
            def _():
                total_of_pair(w - length)

        @pl.when(within(w - (length - 1)))
        def _():
            total_of_line(w - (length - 1))

        def reduce_step(k):
            t = length - 2 - k

            @pl.when(within(w - t))
            def _():
                along(w - t, t)

        loop(length - 1, reduce_step)

    loop(chunks + 2 * length, wave)

    def from_core(s):
        def take(i):
            for yy in range(2):
                gc_copy(s, i, yy, 1 - c).wait_recv()
                use(s, at(i, yy, 1 - c))

        for_z(take)

    def last(s):
        def take(i):
            gy_copy(s, i, 1 - y).wait_recv()
            gc_copy(s, i, 1 - y, c).start()
            use(s, at(i, 1 - y, c))

        @pl.when(jnp.logical_not(line_first(s)))
        def _():
            for_z(take)

        @pl.when(s > 0)
        def _():
            from_core(s - 1)

    loop(chunks, last)
    from_core(chunks - 1)

    def drain(s):
        @pl.when(s >= chunks - 2)
        def _():
            for h in range(2):
                core_copy(s, h).wait_send()

        @pl.when(line_first(s))
        def _():
            pair_one(s).wait_send()
            gy_copy(s, z, y).wait_send()

        @pl.when(jnp.logical_not(line_first(s)))
        def _():
            pair_copy(s).wait_send()
            for_z(lambda i: gy_copy(s, i, y).wait_send())

        def flow(f):
            def step(t):
                for d in range(2):
                    place = z if d == 0 else length - 1 - z
                    origin = z - t if d == 0 else z + t

                    @pl.when((place <= t) & (place < length - 1))
                    def _():
                        line_copy(s, t, d, f).wait_send()

                    @pl.when((origin >= 0) & (origin < length) & (place < length - 1))
                    def _():
                        gz_copy(s, t, d, f).wait_send()

            loop(length - 1, step)

        loop(flows(s), flow)

        def blocks(i):
            for yy in range(2):
                gc_copy(s, i, yy, c).wait_send()

        for_z(blocks)

    loop(chunks, drain)


def outputs_kernel(
    half_total, stat_ref, incl_ref, eta_ref, labels_ref, prior_ref, scale_ref, offset_ref,
    incl_out, mean_out, resid_out,
):
    scale = scale_ref[...]
    shrink = scale / (1.0 + scale)
    bias = prior_ref[...] - 0.5 * jnp.log1p(scale)
    stat = stat_ref[...]
    mean_out[...] = stat * shrink
    logit = bias + (half_total * shrink) * stat * stat
    incl_out[...] = 0.5 * incl_ref[...] + 0.5 * jax.nn.sigmoid(logit)
    resid_out[...] = 4.0 * (
        labels_ref[...].astype(jnp.float32) - jax.nn.sigmoid(eta_ref[...] + offset_ref[...])
    )


def on_device(genotype, residual, labels, incl_old, mean_old, prior_logit, slab_scale, offset):
    n = lax.axis_size("ind")
    people, _ = genotype.shape
    owned, columns = incl_old.shape
    length = n // 4
    chunks = max(1, min(4, owned // 256))
    period = 2 if chunks % 2 == 0 else 0
    slots = chunks + chunks // 2 if period else chunks
    rows = owned // chunks
    f32, bf16, i16 = jnp.float32, jnp.bfloat16, jnp.int16
    anywhere = pl.BlockSpec(memory_space=pl.ANY)
    vmem = pl.BlockSpec(memory_space=pltpu.VMEM)
    dma = pltpu.SemaphoreType.DMA
    hops = length - 1
    prior, scale, shift = (v.reshape(1, -1) for v in (prior_logit, slab_scale, offset))
    stat, eta = pl.pallas_call(
        functools.partial(sweep_kernel, n, chunks, period),
        out_shape=(
            jax.ShapeDtypeStruct((owned, columns), f32),
            jax.ShapeDtypeStruct((people, columns), f32),
        ),
        in_specs=[anywhere, vmem, anywhere, anywhere, vmem, vmem],
        out_specs=(vmem, vmem),
        scratch_shapes=[
            pltpu.VMEM(genotype.shape, bf16),
            pltpu.VMEM(incl_old.shape, f32),
            pltpu.VMEM(mean_old.shape, f32),
            pltpu.VMEM((min(chunks, 2), 2, length, rows, columns), f32),
            pltpu.VMEM((chunks, 2, length, rows, columns), f32),
            pltpu.VMEM((chunks, length, rows, columns), i16),
            pltpu.VMEM((chunks, length, rows, columns), i16),
            pltpu.VMEM((slots, length, rows, columns), f32),
            pltpu.VMEM((slots, hops, 2, rows, columns), i16),
            pltpu.VMEM((slots, hops, 2, rows, columns), i16),
            pltpu.VMEM((chunks, n, rows, columns), bf16),
            dma((chunks, n)),
            dma((2,)),
            dma((chunks, 2)),
            dma((chunks, 2)),
            dma((chunks,)),
            dma((chunks,)),
            dma((slots, hops, 2)),
            dma((slots, hops, 2)),
            dma((slots, hops, 2)),
            dma((slots, hops, 2)),
            dma((chunks, length)),
            dma((chunks, length)),
            dma((chunks, 2, length)),
            dma((chunks, 2, length)),
        ],
        compiler_params=pltpu.CompilerParams(
            collective_id=0, has_side_effects=True, vmem_limit_bytes=67043328
        ),
        name="sweep",
    )(genotype, residual, incl_old, mean_old, prior, scale)

    steps = 4 if owned % 32 == 0 and people % 32 == 0 else 1
    upper = pl.BlockSpec((owned // steps, columns), lambda i: (i, 0))
    lower = pl.BlockSpec((people // steps, columns), lambda i: (i, 0))
    flat = pl.BlockSpec((1, columns), lambda i: (0, 0))
    return pl.pallas_call(
        functools.partial(outputs_kernel, 0.5 * people * n),
        grid=(steps,),
        out_shape=(
            jax.ShapeDtypeStruct((owned, columns), f32),
            jax.ShapeDtypeStruct((owned, columns), f32),
            jax.ShapeDtypeStruct((people, columns), f32),
        ),
        in_specs=[upper, upper, lower, lower, flat, flat, flat],
        out_specs=(upper, upper, lower),
        name="outputs",
    )(stat, incl_old, eta, labels, prior, scale, shift)


def solution(mesh):
    placed = (
        P(("groups", "ind"), None),
        P(("groups", "ind"), None),
        P(("groups", "ind"), None),
        P(("groups", "ind"), None),
        P(("groups", "ind"), None),
        P(),
        P(),
        P(),
    )
    return jax.shard_map(
        on_device,
        mesh=mesh,
        in_specs=placed,
        out_specs=(
            P(("groups", "ind"), None),
            P(("groups", "ind"), None),
            P(("groups", "ind"), None),
        ),
        check_vma=False,
    )
```

```python
import functools
import math

import jax
import jax.numpy as jnp
from jax import lax
from jax.experimental import pallas as pl
from jax.experimental.pallas import tpu as pltpu
from jax.sharding import PartitionSpec as P

LARGEST_TERM = 64.0


def sweep_kernel(
    n, chunks, wide_chunks,
    geno_hbm, resid_ref, incl_hbm, mean_hbm, prior_ref, scale_ref,
    stat_out, eta,
    geno, incl, mean, core_out, core_in, pair_out, pair_in, own, line_out, line_in, eff,
    geno_sem, in_sem, core_ss, core_rs, pair_ss, pair_rs, line_ss, line_rs,
    gz_ss, gz_rs, gy_ss, gy_rs, gc_ss, gc_rs,
):
    length = n // 4
    owned = incl.shape[0]
    rows = owned // chunks
    people = geno.shape[0]
    total = float(people * n)
    coding = 32760.0 / math.log(1.0 + LARGEST_TERM * total)
    me = lax.axis_index("ind")
    z = me // 4
    y = (me // 2) % 2
    c = me % 2

    def at(zz, yy, cc):
        return zz * 4 + yy * 2 + cc

    core_dev = {"ind": at(z, y, 1 - c)}
    pair_dev = {"ind": at(z, 1 - y, c)}
    up_dev = {"ind": at(lax.rem(z + 1, length), y, c)}
    down_dev = {"ind": at(lax.rem(z + length - 1, length), y, c)}
    has_up = z < length - 1
    has_down = z > 0

    def remote(src, dst, ss, rs, dev):
        return pltpu.make_async_remote_copy(
            src_ref=src, dst_ref=dst, send_sem=ss, recv_sem=rs,
            device_id=dev, device_id_type=pl.DeviceIdType.MESH,
        )

    def encode(x):
        code = (jnp.log(1.0 + jnp.abs(x)) * coding + 0.5).astype(jnp.int32)
        return jnp.where(x < 0.0, -code, code).astype(jnp.int16)

    def decode(code):
        level = code.astype(jnp.int32).astype(jnp.float32)
        size = jnp.exp(jnp.abs(level) * (1.0 / coding)) - 1.0
        return jnp.where(level < 0.0, -size, size)

    def cols(s, o):
        return pl.ds(pl.multiple_of(o * owned + s * rows, 128), rows)

    def load(s, o):
        return pltpu.make_async_copy(
            geno_hbm.at[:, cols(s, o)], geno.at[:, cols(s, o)], geno_sem.at[s, o]
        )

    def for_z(body):
        lax.fori_loop(0, length, lambda i, _: (body(i), 0)[1], 0)

    def loop(count, body):
        lax.fori_loop(0, count, lambda i, _: (body(i), 0)[1], 0)

    owners = ((1 - y, 1 - c), (y, 1 - c), (y, c), (1 - y, c))

    def load_chunk(s):
        for yy, cc in owners:
            for_z(lambda i: load(s, at(i, yy, cc)).start())

    loop(chunks, load_chunk)
    small = [
        pltpu.make_async_copy(incl_hbm, incl, in_sem.at[0]),
        pltpu.make_async_copy(mean_hbm, mean, in_sem.at[1]),
    ]
    for copy in small:
        copy.start()

    barrier = pltpu.get_barrier_semaphore()
    pl.semaphore_signal(barrier, inc=1, device_id=core_dev, device_id_type=pl.DeviceIdType.MESH)
    pl.semaphore_signal(barrier, inc=1, device_id=pair_dev, device_id_type=pl.DeviceIdType.MESH)

    @pl.when(has_up)
    def _():
        pl.semaphore_signal(barrier, inc=1, device_id=up_dev, device_id_type=pl.DeviceIdType.MESH)

    @pl.when(has_down)
    def _():
        pl.semaphore_signal(barrier, inc=1, device_id=down_dev, device_id_type=pl.DeviceIdType.MESH)

    pl.semaphore_wait(barrier, 2 + has_up.astype(jnp.int32) + has_down.astype(jnp.int32))

    def product(s, o):
        load(s, o).wait()
        return lax.dot_general(
            geno[:, cols(s, o)], resid_ref[...], (((0,), (0,)), ((), ())),
            preferred_element_type=jnp.float32,
        )

    def wide(s):
        return s >= chunks - wide_chunks

    def side(f):
        return jnp.where(f == 0, y, 1 - y)

    def core_copy(s, h):
        return remote(
            core_out.at[s % 2, h], core_in.at[s, h], core_ss.at[s, h], core_rs.at[s, h], core_dev
        )

    def pair_copy(s):
        return remote(pair_out.at[s], pair_in.at[s], pair_ss.at[s], pair_rs.at[s], pair_dev)

    def line_copy(s, t, d):
        return remote(
            line_out.at[s, t, d], line_in.at[s, t, d], line_ss.at[s, t, d], line_rs.at[s, t, d],
            up_dev if d == 0 else down_dev,
        )

    def first(s):
        def to_core(h):
            yy, cc = owners[h]

            @pl.when(s >= 2)
            def _():
                core_copy(s - 2, h).wait_send()

            def part(i):
                core_out[s % 2, h, i] = product(s, at(i, yy, cc))

            for_z(part)
            core_copy(s, h).start()

        to_core(0)

        def keep(i):
            own[s, i] = product(s, at(i, y, c))

        for_z(keep)
        core_copy(s, 0).wait_recv()

        def pass_on(i):
            pair_out[s, i] = encode(product(s, at(i, 1 - y, c)) + core_in[s, 0, i])

        for_z(pass_on)
        pair_copy(s).start()
        to_core(1)

    loop(chunks, first)
    for copy in small:
        copy.wait()
    eta[...] = jnp.zeros_like(eta)

    scale = scale_ref[...]
    shrink = scale / (1.0 + scale)
    bias = prior_ref[...] - 0.5 * jnp.log1p(scale)
    curve = 0.5 * total * shrink

    def along(s, t):
        @pl.when(t == 0)
        def _():
            core_copy(s, 1).wait_recv()
            pair_copy(s).wait_recv()

            def add(i):
                own[s, i] = own[s, i] + core_in[s, 1, i] + decode(pair_in[s, i])

            for_z(add)

        for d in range(2):
            place = z if d == 0 else length - 1 - z
            block = length - 1 - t + z if d == 0 else t - (length - 1 - z)

            @pl.when((place <= t) & (place < length - 1))
            def _():
                @pl.when(place == 0)
                def _():
                    line_out[s, t, d] = encode(own[s, block])

                @pl.when(place > 0)
                def _():
                    line_copy(s, t - 1, d).wait_recv()
                    line_out[s, t, d] = encode(own[s, block] + decode(line_in[s, t - 1, d]))

                line_copy(s, t, d).start()

    def gz_copy(s, u, d, f):
        k, o = 2 * s + f, at(z - u if d == 0 else z + u, side(f), c)
        return remote(
            eff.at[s, o], eff.at[s, o], gz_ss.at[k, u, d], gz_rs.at[k, u, d], up_dev if d == 0 else down_dev
        )

    def gz_landed(s, u, d, f):
        k, o = 2 * s + f, at(z - 1 - u if d == 0 else z + 1 + u, side(f), c)
        return remote(
            eff.at[s, o], eff.at[s, o], gz_ss.at[k, u, d], gz_rs.at[k, u, d], up_dev if d == 0 else down_dev
        )

    def gy_copy(s, i, yy):
        o = at(i, yy, c)
        return remote(eff.at[s, o], eff.at[s, o], gy_ss.at[s, i], gy_rs.at[s, i], pair_dev)

    def gc_copy(s, i, yy, cc):
        o = at(i, yy, cc)
        return remote(eff.at[s, o], eff.at[s, o], gc_ss.at[s, yy, i], gc_rs.at[s, yy, i], core_dev)

    def use(s, o):
        eta[...] += jnp.dot(geno[:, cols(s, o)], eff[s, o], preferred_element_type=jnp.float32)

    def send_own(s, f):
        @pl.when(has_up)
        def _():
            gz_copy(s, 0, 0, f).start()

        @pl.when(has_down)
        def _():
            gz_copy(s, 0, 1, f).start()

        gc_copy(s, z, side(f), c).start()

    def finish(s):
        for d in range(2):
            @pl.when(has_down if d == 0 else has_up)
            def _():
                line_copy(s, length - 2, d).wait_recv()
                own[s, z] = own[s, z] + decode(line_in[s, length - 2, d])

        here = pl.ds(pl.multiple_of(s * rows, 8), rows)
        before = incl[here, :]
        stat = own[s, z] / total + before * mean[here, :]
        stat_out[here, :] = stat
        incl_new = 0.5 * before + 0.5 * jax.nn.sigmoid(bias + curve * stat * stat)
        eff[s, me] = (incl_new * (stat * shrink)).astype(jnp.bfloat16)
        gy_copy(s, z, y).start()
        send_own(s, 0)
        use(s, me)

    def send_other(s):
        gy_copy(s, z, 1 - y).wait_recv()
        send_own(s, 1)
        use(s, at(z, 1 - y, c))

    def spread(s, u, f):
        for d in range(2):
            source = z - u if d == 0 else z + u

            @pl.when((source >= 0) & (source < length))
            def _():
                gz_landed(s, u - 1, d, f).wait_recv()

                @pl.when(has_up if d == 0 else has_down)
                def _():
                    gz_copy(s, u, d, f).start()

                @pl.when(jnp.logical_not(wide(s)))
                def _():
                    gy_copy(s, source, y).start()

                gc_copy(s, source, side(f), c).start()
                use(s, at(source, side(f), c))

    def within(s):
        return (s >= 0) & (s < chunks)

    def from_core(s):
        def take(i):
            for yy in range(2):
                gc_copy(s, i, yy, 1 - c).wait_recv()
                use(s, at(i, yy, 1 - c))

        for_z(take)

    def last(s):
        def take(i):
            gy_copy(s, i, 1 - y).wait_recv()
            gc_copy(s, i, 1 - y, c).start()
            use(s, at(i, 1 - y, c))

        @pl.when(jnp.logical_not(wide(s)))
        def _():
            for_z(take)

        @pl.when(s > 0)
        def _():
            from_core(s - 1)

    def wave(w):
        def gather_step(k):
            u = length - 1 - k
            s = w - (length - 1) - u

            @pl.when(within(s - 1) & wide(s - 1))
            def _():
                spread(s - 1, u, 1)

            @pl.when(within(s))
            def _():
                spread(s, u, 0)

        loop(length - 1, gather_step)
        here = w - (length - 1)

        @pl.when(within(here - 1) & wide(here - 1))
        def _():
            send_other(here - 1)

        @pl.when(within(here))
        def _():
            finish(here)

        def reduce_step(k):
            t = length - 2 - k

            @pl.when(within(w - t))
            def _():
                along(w - t, t)

        loop(length - 1, reduce_step)

        @pl.when(within(w - 2 * length + 1))
        def _():
            last(w - 2 * length + 1)

    loop(chunks + 2 * length - 1, wave)
    from_core(chunks - 1)

    def drain(s):
        @pl.when(s >= chunks - 2)
        def _():
            for h in range(2):
                core_copy(s, h).wait_send()

        pair_copy(s).wait_send()
        gy_copy(s, z, y).wait_send()

        @pl.when(jnp.logical_not(wide(s)))
        def _():
            def sent(i):
                @pl.when(i != z)
                def _():
                    gy_copy(s, i, y).wait_send()

            for_z(sent)

        def step(t):
            for d in range(2):
                place = z if d == 0 else length - 1 - z
                origin = z - t if d == 0 else z + t

                @pl.when((place <= t) & (place < length - 1))
                def _():
                    line_copy(s, t, d).wait_send()

                @pl.when((origin >= 0) & (origin < length) & (place < length - 1))
                def _():
                    gz_copy(s, t, d, 0).wait_send()

                    @pl.when(wide(s))
                    def _():
                        gz_copy(s, t, d, 1).wait_send()

        loop(length - 1, step)

        def blocks(i):
            for yy in range(2):
                gc_copy(s, i, yy, c).wait_send()

        for_z(blocks)

    loop(chunks, drain)


def outputs_kernel(
    half_total, stat_ref, incl_ref, eta_ref, labels_ref, prior_ref, scale_ref, offset_ref,
    incl_out, mean_out, resid_out,
):
    scale = scale_ref[...]
    shrink = scale / (1.0 + scale)
    bias = prior_ref[...] - 0.5 * jnp.log1p(scale)
    stat = stat_ref[...]
    mean_out[...] = stat * shrink
    logit = bias + (half_total * shrink) * stat * stat
    incl_out[...] = 0.5 * incl_ref[...] + 0.5 * jax.nn.sigmoid(logit)
    resid_out[...] = 4.0 * (
        labels_ref[...].astype(jnp.float32) - jax.nn.sigmoid(eta_ref[...] + offset_ref[...])
    )


def on_device(genotype, residual, labels, incl_old, mean_old, prior_logit, slab_scale, offset):
    n = lax.axis_size("ind")
    people, _ = genotype.shape
    owned, columns = incl_old.shape
    length = n // 4
    chunks = max(1, min(4, owned // 256))
    wide_chunks = 0
    rows = owned // chunks
    f32, bf16, i16 = jnp.float32, jnp.bfloat16, jnp.int16
    anywhere = pl.BlockSpec(memory_space=pl.ANY)
    vmem = pl.BlockSpec(memory_space=pltpu.VMEM)
    dma = pltpu.SemaphoreType.DMA
    hops = length - 1
    prior, scale, shift = (v.reshape(1, -1) for v in (prior_logit, slab_scale, offset))
    stat, eta = pl.pallas_call(
        functools.partial(sweep_kernel, n, chunks, wide_chunks),
        out_shape=(
            jax.ShapeDtypeStruct((owned, columns), f32),
            jax.ShapeDtypeStruct((people, columns), f32),
        ),
        in_specs=[anywhere, vmem, anywhere, anywhere, vmem, vmem],
        out_specs=(vmem, vmem),
        scratch_shapes=[
            pltpu.VMEM(genotype.shape, bf16),
            pltpu.VMEM(incl_old.shape, f32),
            pltpu.VMEM(mean_old.shape, f32),
            pltpu.VMEM((min(chunks, 2), 2, length, rows, columns), f32),
            pltpu.VMEM((chunks, 2, length, rows, columns), f32),
            pltpu.VMEM((chunks, length, rows, columns), i16),
            pltpu.VMEM((chunks, length, rows, columns), i16),
            pltpu.VMEM((chunks, length, rows, columns), f32),
            pltpu.VMEM((chunks, hops, 2, rows, columns), i16),
            pltpu.VMEM((chunks, hops, 2, rows, columns), i16),
            pltpu.VMEM((chunks, n, rows, columns), bf16),
            dma((chunks, n)),
            dma((2,)),
            dma((chunks, 2)),
            dma((chunks, 2)),
            dma((chunks,)),
            dma((chunks,)),
            dma((chunks, hops, 2)),
            dma((chunks, hops, 2)),
            dma((2 * chunks, hops, 2)),
            dma((2 * chunks, hops, 2)),
            dma((chunks, length)),
            dma((chunks, length)),
            dma((chunks, 2, length)),
            dma((chunks, 2, length)),
        ],
        compiler_params=pltpu.CompilerParams(
            collective_id=0, has_side_effects=True, vmem_limit_bytes=67043328
        ),
        name="sweep",
    )(genotype, residual, incl_old, mean_old, prior, scale)

    steps = 4 if owned % 32 == 0 and people % 32 == 0 else 1
    upper = pl.BlockSpec((owned // steps, columns), lambda i: (i, 0))
    lower = pl.BlockSpec((people // steps, columns), lambda i: (i, 0))
    flat = pl.BlockSpec((1, columns), lambda i: (0, 0))
    return pl.pallas_call(
        functools.partial(outputs_kernel, 0.5 * people * n),
        grid=(steps,),
        out_shape=(
            jax.ShapeDtypeStruct((owned, columns), f32),
            jax.ShapeDtypeStruct((owned, columns), f32),
            jax.ShapeDtypeStruct((people, columns), f32),
        ),
        in_specs=[upper, upper, lower, lower, flat, flat, flat],
        out_specs=(upper, upper, lower),
        name="outputs",
    )(stat, incl_old, eta, labels, prior, scale, shift)


def solution(mesh):
    placed = (
        P(("groups", "ind"), None),
        P(("groups", "ind"), None),
        P(("groups", "ind"), None),
        P(("groups", "ind"), None),
        P(("groups", "ind"), None),
        P(),
        P(),
        P(),
    )
    return jax.shard_map(
        on_device,
        mesh=mesh,
        in_specs=placed,
        out_specs=(
            P(("groups", "ind"), None),
            P(("groups", "ind"), None),
            P(("groups", "ind"), None),
        ),
        check_vma=False,
    )
```
